32 devices in a mesh: blk: 16 (over z, y, core), map: 2 (over x).
Axes of the slice: x: 2, y: 2, z: 4, core: 2. Of those that a mesh axis runs over, the one named last changes fastest.
Arguments:
- phase_history: bfloat16 [16, 2, 128, 1024], P('blk', 'map'), may hold values from -6 to 6
- tile_curvature: float32 [16], P('blk'), may hold values from 20 to 80
- interp_weights: bfloat16 [16, 512, 512], P('blk'), may hold values from -0.25 to 0.25
- strip_tiles: int32 [16, 2, 256, 1], P('blk', 'map'), may hold values from 0 to 15; in each aligned block of 256 rows (0 to 255, 256 to 511, ..., all dimensions but the last counted through in order) at most 32 rows name the same one
- row_offsets: int32 [16, 2, 256], P('blk', 'map'), may hold values from 0 to 255
- tile_owner: int32 [16], replicated, may hold values from 0 to 15, each once
Outputs:
- map_power: float32 [16, 2, 256, 512], P('blk', 'map')
The draws below stay inside these ranges and needn't reach their ends.
Inputs may be any that keep to these rules, and one draw needn't show every extreme that they name: `strip_tiles`: among the rows of one device no map tile is named more than 32 times, and in every draw some device names some tile exactly 32 times. `tile_owner`: every blk index holds exactly one map tile.
All inputs are finite; a program needn't handle non-finite values.
Results may differ from the reference program's by a relative error of at most 0.0055.
Values may be sent and summed in bfloat16 or wider, within the bound.
A program may use at most 64 MiB of HBM per device.

```python
import math
import jax
import jax.numpy as jnp
import numpy as np
from jax import lax

NB = 128
NF = 512
TR = 512
TC = 512
STOPS = 8
MAPH = 256
ROWS_DEV = 256
CAP = 32
N_BLK = 16
N_MAP = 2


def place_ends(result, own_key, low, largest):
    longest = result.shape.index(max(result.shape))
    spots = []
    for shift in (0, 1):
        where = [jax.random.randint(jax.random.fold_in(own_key, axis), (), 0, length) for axis, length in enumerate(result.shape)]
        where[longest] = (where[longest] + shift) % result.shape[longest]
        spots.append(tuple(where))
    return result.at[spots[0]].set(low).at[spots[1]].set(largest)


def levels(stream_key, shape, split, least, high):
    level = 1.0
    for dim, shards_of in split:
        draws = jax.random.uniform(jax.random.fold_in(jax.random.fold_in(stream_key, 6), dim), (shards_of,), jnp.float32, least / len(split), high / len(split))
        level = level * jnp.repeat(jnp.exp(draws), shape[dim] // shards_of).reshape((-1,) + (1,) * (len(shape) - 1 - dim))
    return level


def assign_block(key, own, number, rows, count, top, limit, slope):
    ranking = jax.random.permutation(key, count)
    crowded, common = load_shares(count, rows * top, limit, slope, True), load_shares(count, rows * top, limit, slope, False)
    places = jnp.arange(count)

    def named(sizes, rotation):
        used = int((sizes > 0).sum())
        fixed = max(1, used // 4)
        passed = fixed + (places - fixed + rotation * (used - fixed)) % max(1, count - fixed)
        return jnp.zeros((count,), jnp.int32).at[ranking[jnp.where(places < fixed, places, passed)]].set(jnp.asarray(sizes, jnp.int32))

    sizes = jnp.where(number % 4 == 0, named(crowded, number // 4), named(common, number - number // 4 - 1))
    mixed = jax.random.permutation(jax.random.fold_in(own, 3), count)
    donor, taker = mixed[0:count // 2 * 2:2], mixed[1:count // 2 * 2:2]
    room = jnp.minimum(sizes[donor] - 1, limit - sizes[taker]) // 2
    room = jnp.where((donor == ranking[0]) | (taker == ranking[0]) | (sizes[taker] == 0), 0, jnp.maximum(room, 0))
    passed = jax.random.randint(jax.random.fold_in(own, 4), (count // 2,), 0, 1 << 20) % (room + 1)
    sizes = sizes.at[donor].add(-passed).at[taker].add(passed)
    members = jnp.searchsorted(jnp.cumsum(sizes), jnp.arange(rows * top), side="right").astype(jnp.int32)
    grid = members.reshape(top, rows).T
    grid = grid[jax.random.permutation(jax.random.fold_in(own, 1), rows)]
    rotation = jax.random.randint(jax.random.fold_in(own, 2), (rows, 1), 0, top)
    return jnp.take_along_axis(grid, (jnp.arange(top)[None, :] + rotation) % top, axis=1)


def load_shares(count, total, most, skew, full):
    weights = [(1 << 20) // math.isqrt(rank ** skew) + 1 for rank in range(1, count + 1)]
    largest = most if full else min(most, max(-(-total // count), total * weights[0] // sum(weights)))
    least = 1 if total - largest >= count - 1 else 0
    given, surplus = [largest] + [least] * (count - 1), total - largest - least * (count - 1)
    while surplus > 0:
        free = [i for i in range(1, count) if given[i] < largest] or [i for i in range(1, count) if given[i] < most]
        mass, left = sum([weights[i] for i in free]), surplus
        for i in free:
            addition = min(most - given[i], max(1, left * weights[i] // mass), surplus)
            given[i] = given[i] + addition
            surplus = surplus - addition
    return np.array(given)


def normal_values(own_key, shape, width, most, cuts=(), kind=jnp.bfloat16):
    drawn = width * jax.random.normal(own_key, shape, jnp.float32)
    if cuts:
        drawn = drawn * levels(own_key, shape, cuts, -0.22, 0.18)
    return jnp.clip(drawn, -most, most).astype(kind)


def setup_inputs(seed: int = 0) -> dict:
    key_of = jax.random.split(jax.random.key(seed), 7)
    phase_history = normal_values(key_of[0], (N_BLK, N_MAP, NB, 2 * NF), 1.0, 6.0, ((0, 16), (1, 2)))
    tile_curvature = jnp.clip(20.0 + 60.0 * jax.random.uniform(key_of[1], (N_BLK,), jnp.float32) ** levels(key_of[1], (N_BLK,), ((0, 16),), -0.2, 0.2), 20.0, 80.0)
    interp_weights = normal_values(key_of[2], (N_BLK, TC, TC), TC ** -0.5, 0.25, ((0, 16),))
    strip_tiles_keys = jax.random.split(jax.random.fold_in(key_of[3], 1), N_BLK * N_MAP * ROWS_DEV // ROWS_DEV)
    strip_tiles_turns = jax.random.permutation(jax.random.fold_in(key_of[3], 3), N_BLK * N_MAP * ROWS_DEV // ROWS_DEV)
    strip_tiles = jax.vmap(lambda own, number: assign_block(jax.random.fold_in(key_of[3], 2), own, number, ROWS_DEV, N_BLK, 1, CAP, 2))(strip_tiles_keys, strip_tiles_turns).reshape((N_BLK, N_MAP, ROWS_DEV, 1))
    row_offsets = place_ends(jax.random.randint(key_of[4], (N_BLK, N_MAP, ROWS_DEV), 0, MAPH), jax.random.fold_in(key_of[4], 1), 0, MAPH - 1).astype(jnp.int32)
    tile_owner = jax.random.permutation(key_of[5], N_BLK).astype(jnp.int32)
    return {"phase_history": phase_history, "tile_curvature": tile_curvature, "interp_weights": interp_weights, "strip_tiles": strip_tiles, "row_offsets": row_offsets, "tile_owner": tile_owner}


def range_matrix(freq_count, column_count):
    freq_index = jnp.arange(freq_count, dtype=jnp.int32)[:, None]
    column_index = jnp.arange(column_count, dtype=jnp.int32)[None, :]
    angle = (freq_index * column_index % freq_count).astype(jnp.float32) * (2.0 * math.pi / freq_count)
    factor = 1.0 / math.sqrt(freq_count)
    real_part = jnp.cos(angle) * factor
    imag_part = -jnp.sin(angle) * factor
    upper = jnp.concatenate([real_part, imag_part], axis=1)
    lower = jnp.concatenate([-imag_part, real_part], axis=1)
    return jnp.concatenate([upper, lower], axis=0).astype(jnp.bfloat16)

def cross_rows(stop_index, map_index, row_index, map_count, pulse_count, span):
    pulse_index = jnp.arange(pulse_count, dtype=jnp.int32)[None, :]
    along = (stop_index * map_count + map_index) * pulse_count + pulse_index
    angle = (row_index[:, None] * along % span).astype(jnp.float32) * (2.0 * math.pi / span)
    factor = 1.0 / math.sqrt(span)
    return jnp.concatenate([jnp.cos(angle) * factor, -jnp.sin(angle) * factor], axis=1).astype(jnp.bfloat16)

def apply_phase(source_block, curvature, stop_index, map_index, map_count, pulse_count, freq_count, span):
    pulse_index = jnp.arange(pulse_count, dtype=jnp.int32)
    along = ((stop_index * map_count + map_index) * pulse_count + pulse_index).astype(jnp.float32) / span - 0.5
    relative = jnp.arange(freq_count, dtype=jnp.int32).astype(jnp.float32) / freq_count - 0.5
    phase_angle = curvature * (along * along)[:, None] * (1.0 + relative[None, :])
    cosine = jnp.cos(phase_angle)
    sine = jnp.sin(phase_angle)
    values = source_block.astype(jnp.float32)
    real_part = values[:, :freq_count]
    imag_part = values[:, freq_count:]
    return jnp.concatenate([real_part * cosine - imag_part * sine, real_part * sine + imag_part * cosine], axis=1).astype(jnp.bfloat16)

def stack_spectrum(spectrum_now):
    half_width = spectrum_now.shape[1] // 2
    real_part = spectrum_now[:, :half_width]
    imag_part = spectrum_now[:, half_width:]
    upper = jnp.concatenate([real_part, imag_part], axis=1)
    lower = jnp.concatenate([-imag_part, real_part], axis=1)
    return jnp.concatenate([upper, lower], axis=0)

def tile_image(tile_index, phase_history, curvature):
    lead_count = STOPS // 2 - 1
    span = STOPS * N_MAP * NB
    ranges = range_matrix(NF, TC).astype(jnp.float32)
    row_index = jnp.arange(TR, dtype=jnp.int32)
    running = jnp.zeros((TR, 2 * TC), jnp.float32)
    for stop_index in range(STOPS):
        source = ((tile_index + stop_index - lead_count) % N_BLK).astype(jnp.int32)
        column_blocks = lax.dynamic_index_in_dim(phase_history, source, 0, keepdims=False)
        for map_index in range(N_MAP):
            phased = apply_phase(column_blocks[map_index], curvature, stop_index, map_index, N_MAP, NB, NF, span)
            spectrum_now = jnp.dot(phased.astype(jnp.float32), ranges, precision=lax.Precision.HIGHEST).astype(jnp.bfloat16)
            crossing = cross_rows(stop_index, map_index, row_index, N_MAP, NB, span).astype(jnp.float32)
            running = running + jnp.dot(crossing, stack_spectrum(spectrum_now).astype(jnp.float32), precision=lax.Precision.HIGHEST)
    return running.astype(jnp.bfloat16)

def reference(phase_history, tile_curvature, interp_weights, strip_tiles, row_offsets, tile_owner):

    def one_tile(tile_index):
        return tile_image(tile_index, phase_history, tile_curvature[tile_index])
    images = lax.map(one_tile, jnp.arange(N_BLK, dtype=jnp.int32))
    strip_rows = images.reshape(N_BLK, N_MAP, ROWS_DEV, 2 * TC)
    destination = tile_owner[strip_tiles[..., 0]].astype(jnp.int32)
    slot_count = N_BLK * CAP
    results = []
    for map_index in range(N_MAP):
        flat_rows = strip_rows[:, map_index].reshape(N_BLK * ROWS_DEV, 2 * TC)
        flat_dest = destination[:, map_index].reshape(N_BLK * ROWS_DEV)
        flat_offsets = row_offsets[:, map_index].reshape(N_BLK * ROWS_DEV).astype(jnp.int32)
        sorted_rows = jnp.argsort(flat_dest, stable=True).astype(jnp.int32)
        holder_counts = lax.optimization_barrier(jnp.sum((flat_dest[:, None] == jnp.arange(N_BLK, dtype=jnp.int32)[None, :]).astype(jnp.int32), axis=0)).astype(jnp.int32)
        holder_starts = (jnp.cumsum(holder_counts) - holder_counts).astype(jnp.int32)
        padded_rows = jnp.concatenate([sorted_rows, jnp.zeros((slot_count,), jnp.int32)])

        def one_holder(holder):
            picked = lax.dynamic_slice_in_dim(padded_rows, holder_starts[holder], slot_count)
            usable = jnp.arange(slot_count, dtype=jnp.int32) < holder_counts[holder]
            chosen = flat_rows[picked].astype(jnp.float32)
            weights = interp_weights[holder].astype(jnp.float32)
            real_out = jnp.dot(chosen[:, :TC], weights, precision=lax.Precision.HIGHEST)
            imag_out = jnp.dot(chosen[:, TC:], weights, precision=lax.Precision.HIGHEST)
            power_rows = real_out * real_out + imag_out * imag_out
            target = jnp.where(usable, flat_offsets[picked], MAPH).astype(jnp.int32)
            return jnp.zeros((MAPH, TC), jnp.float32).at[target].add(power_rows, mode='drop')
        results.append(lax.map(one_holder, jnp.arange(N_BLK, dtype=jnp.int32)))
    return jnp.stack(results, axis=1)
```

```python
import functools
import math

import jax
import jax.numpy as jnp
import numpy as np
from jax import lax
from jax.experimental import pallas as pl
from jax.experimental.pallas import tpu as pltpu
from jax.sharding import PartitionSpec as P

STOPS = 8
MAPH = 256
LANES = 128
TILE = 16


def fit_turns():
    z = 0.125 - 0.125 * np.cos(np.pi * (np.arange(400) + 0.5) / 400)
    t = np.sqrt(z)
    cheb = np.polynomial.chebyshev.Chebyshev
    cos_fit = cheb.fit(z, np.cos(2 * np.pi * t), 7, domain=[0, 0.25])
    sin_fit = cheb.fit(z, np.sin(2 * np.pi * t) / t, 6, domain=[0, 0.25])
    power = np.polynomial.Polynomial
    return (
        [float(np.float32(c)) for c in cos_fit.convert(kind=power).coef],
        [float(np.float32(c)) for c in sin_fit.convert(kind=power).coef],
    )


COS_COEF, SIN_COEF = fit_turns()


def cos_sin_turns(turns):
    t = turns - jnp.round(turns)
    z = t * t
    c = jnp.full_like(z, COS_COEF[-1])
    for coef in COS_COEF[-2::-1]:
        c = c * z + coef
    s = jnp.full_like(z, SIN_COEF[-1])
    for coef in SIN_COEF[-2::-1]:
        s = s * z + coef
    return c, s * t


def iota(shape, axis):
    return lax.broadcasted_iota(jnp.int32, shape, axis)


def kernel(
    sizes,
    block_ref, curv_ref, weight_ref, tiles_ref, offs_ref, owner_ref,
    out_ref,
    blocks, ranges, cross, phased, right, x_send, x_recv, x_own, packed, arrived, slot_hot,
    o_send, o_recv, u_acc, v_acc,
    g_send, g_recv, xs_sem, xr_sem, as_sem, ar_sem, os_sem, or_sem,
):
    blk, maps, pulses, freqs, columns, rows, cap = sizes
    f32, bf16 = jnp.float32, jnp.bfloat16
    me = lax.axis_index("blk")
    my_map = lax.axis_index("map")
    other_map = 1 - my_map
    core = lax.rem(me, 2)
    span = STOPS * maps * pulses
    stacked = STOPS * pulses
    chunks = columns // LANES
    width = 2 * LANES
    slots = blk * cap
    own_stop = STOPS // 2 - 1

    def device(index):
        return (lax.rem(index + 2 * blk, blk), my_map)

    mesh_id = pl.DeviceIdType.MESH

    barrier = pltpu.get_barrier_semaphore()

    def greet(i, _):
        pl.semaphore_signal(barrier, inc=1, device_id=device(me + i), device_id_type=mesh_id)
        return 0

    lax.fori_loop(1, blk, greet, 0)
    pl.semaphore_signal(barrier, inc=1, device_id=(me, other_map), device_id_type=mesh_id)
    blocks[own_stop] = block_ref[...]
    pl.semaphore_wait(barrier, blk)

    def push(source, stop, target, sem):
        return pltpu.make_async_remote_copy(
            src_ref=source, dst_ref=blocks.at[stop], send_sem=g_send.at[sem],
            recv_sem=g_recv.at[stop], device_id=target, device_id_type=mesh_id)

    def arrived_block(stop):
        pltpu.make_async_copy(blocks.at[stop], blocks.at[stop], g_recv.at[stop]).wait()

    partner = device(me + 1 - 2 * core)
    shift = 2 * core - 1

    push(block_ref, 7, device(me - 4), 0).start()

    @pl.when(core == 1)
    def _():
        push(block_ref, 0, device(me + 3), 6).start()

    push(block_ref, 5, device(me - 2), 1).start()
    push(block_ref, 1, device(me + 2), 2).start()
    push(block_ref, own_stop + shift, partner, 3).start()

    def fill_ranges(i, _):
        at = pl.ds(pl.multiple_of(i * TILE, TILE), TILE)
        below = pl.ds(pl.multiple_of(freqs + i * TILE, TILE), TILE)
        f = (i * TILE + iota((TILE, columns), 0)).astype(f32)
        c = iota((TILE, columns), 1).astype(f32)
        re, im = cos_sin_turns(f * c * (1.0 / freqs))
        re = (re * (1.0 / math.sqrt(freqs))).astype(bf16)
        im = (im * (1.0 / math.sqrt(freqs)))
        pos, neg = im.astype(bf16), (-im).astype(bf16)
        for n in range(chunks):
            cut = slice(n * LANES, (n + 1) * LANES)
            ranges[n, at, 0:LANES] = re[:, cut]
            ranges[n, at, LANES:width] = neg[:, cut]
            ranges[n, below, 0:LANES] = pos[:, cut]
            ranges[n, below, LANES:width] = re[:, cut]
        return 0

    lax.fori_loop(0, freqs // TILE, fill_ranges, 0)

    curvature = curv_ref[0]

    def spectrum(k):
        first = (k * maps + my_map) * pulses

        def turn(i, _):
            at = pl.ds(pl.multiple_of(i * TILE, TILE), TILE)
            q = first + i * TILE + iota((TILE, freqs), 0)
            s = q.astype(f32) * (1.0 / span) - 0.5
            r = iota((TILE, freqs), 1).astype(f32) * (1.0 / freqs) - 0.5
            angle = curvature * (s * s) * (1.0 + r)
            c, si = cos_sin_turns(angle * (0.5 / math.pi))
            re = blocks[k, at, 0:freqs].astype(f32)
            im = blocks[k, at, freqs:2 * freqs].astype(f32)
            phased[at, 0:freqs] = (re * c - im * si).astype(bf16)
            phased[at, freqs:2 * freqs] = (re * si + im * c).astype(bf16)
            return 0

        lax.fori_loop(0, pulses // TILE, turn, 0)
        top = pl.ds(pl.multiple_of(k * pulses, pulses), pulses)
        low = pl.ds(pl.multiple_of(stacked + k * pulses, pulses), pulses)

        def chunk(n, _):
            y = jnp.dot(phased[...], ranges[n], preferred_element_type=f32)
            yr, yi = y[:, :LANES], y[:, LANES:]
            right[n, top, 0:LANES] = yr.astype(bf16)
            right[n, top, LANES:width] = yi.astype(bf16)
            right[n, low, 0:LANES] = (-yi).astype(bf16)
            right[n, low, LANES:width] = yr.astype(bf16)
            return 0

        lax.fori_loop(0, chunks, chunk, 0)

    def fill_cross():
        lane = iota((1, stacked), 1)
        q = (lane + (lax.div(lane, pulses) * (maps - 1) + my_map) * pulses).astype(f32)

        def fill(i, _):
            at = pl.ds(pl.multiple_of(i * TILE, TILE), TILE)
            a = (i * TILE + iota((TILE, stacked), 0)).astype(f32)
            re, im = cos_sin_turns(a * q * (1.0 / span))
            cross[at, 0:stacked] = (re * (1.0 / math.sqrt(span))).astype(bf16)
            cross[at, stacked:2 * stacked] = (im * (-1.0 / math.sqrt(span))).astype(bf16)
            return 0

        lax.fori_loop(0, rows * maps // TILE, fill, 0)

    def fill_slots():
        tiles = tiles_ref[...]
        holders = iota((blk, rows), 0)
        dest = jnp.sum(jnp.where(holders == tiles, owner_ref[...], 0), axis=0, keepdims=True)
        hot = (holders == dest).astype(f32)
        upto = (iota((rows, rows), 0) <= iota((rows, rows), 1)).astype(f32).astype(bf16)
        counts = jnp.dot(hot.astype(bf16), upto, preferred_element_type=f32)
        rank = jnp.sum(counts * hot, axis=0, keepdims=True).astype(jnp.int32) - 1
        slot = dest * cap + rank
        for i in range(slots // LANES):
            at = i * LANES + iota((LANES, rows), 0)
            slot_hot[i * LANES:(i + 1) * LANES, :] = (at == slot).astype(f32).astype(bf16)
        place = lax.rem(me, LANES // cap) * cap + rank
        marks = jnp.where(iota((LANES, rows), 0) == place, (offs_ref[...] + 1).astype(f32), 0.0)
        table = lax.dot_general(
            hot.astype(bf16), marks.astype(bf16), (((1,), (1,)), ((), ())),
            preferred_element_type=f32)
        for d in range(blk):
            o_send[d] = table[d:d + 1, :]
        o_recv[me] = o_send[me]

        def send(i, _):
            to = lax.rem(me + i, blk)
            pltpu.make_async_remote_copy(
                src_ref=o_send.at[to], dst_ref=o_recv.at[me], send_sem=os_sem,
                recv_sem=or_sem, device_id=(to, my_map), device_id_type=mesh_id).start()
            return 0

        lax.fori_loop(1, blk, send, 0)

    def step(i, _):
        k = jnp.where(i == 0, own_stop, 0)
        for at, stop in ((1, 4 - 2 * core), (2, 5), (3, 1), (4, 2 + 2 * core), (5, 7), (7, 6)):
            k = jnp.where(i == at, stop, k)

        @pl.when(i == 2)
        def _():
            arrived_block(5)
            push(blocks.at[5], 5 + shift, partner, 4).start()
            arrived_block(1)
            push(blocks.at[1], 1 + shift, partner, 5).start()

        @pl.when(i == 4)
        def _():
            arrived_block(7)

            @pl.when(core == 0)
            def _():
                push(blocks.at[7], 6, partner, 6).start()

        @pl.when((i == 1) | (i == 4) | (i == 6) | (i == 7))
        def _():
            arrived_block(k)

        spectrum(k)

        @pl.when(i == 0)
        def _():
            fill_slots()

        @pl.when(i == 1)
        def _():
            fill_cross()

        return 0

    lax.fori_loop(0, STOPS, step, 0)

    def x_copy(n):
        return pltpu.make_async_remote_copy(
            src_ref=x_send.at[n], dst_ref=x_recv.at[n], send_sem=xs_sem.at[n],
            recv_sem=xr_sem.at[n], device_id=(me, other_map), device_id_type=mesh_id)

    own_slots = pl.ds(pl.multiple_of(me * cap, cap), cap)

    def column_step(n, _):
        @pl.when(n < chunks)
        def _():
            theirs = cross[pl.ds(pl.multiple_of(other_map * rows, rows), rows), :]
            x_send[n] = jnp.dot(theirs, right[n], preferred_element_type=f32).astype(bf16)
            x_copy(n).start()
            mine = cross[pl.ds(pl.multiple_of(my_map * rows, rows), rows), :]
            x_own[n] = jnp.dot(mine, right[n], preferred_element_type=f32)

        @pl.when(n >= 1)
        def _():
            b = n - 1
            x_copy(b).wait_recv()
            image = (x_own[b] + x_recv[b].astype(f32)).astype(bf16)
            packed[b] = jnp.dot(slot_hot[...], image, preferred_element_type=f32).astype(bf16)

            def send(i, _):
                to = lax.rem(me + i, blk)
                pltpu.make_async_remote_copy(
                    src_ref=packed.at[b, pl.ds(pl.multiple_of(to * cap, cap), cap)],
                    dst_ref=arrived.at[b, own_slots], send_sem=as_sem.at[b],
                    recv_sem=ar_sem.at[b], device_id=(to, my_map),
                    device_id_type=mesh_id).start()
                return 0

            lax.fori_loop(1, blk, send, 0)
            arrived[b, own_slots, :] = packed[b, own_slots, :]

        return 0

    lax.fori_loop(0, chunks + 1, column_step, 0)

    def wait_bytes(ref, sem):
        pltpu.make_async_copy(ref, ref, sem).wait()

    others = pl.ds(0, (blk - 1) * cap)
    u_acc[...] = jnp.zeros_like(u_acc)
    v_acc[...] = jnp.zeros_like(v_acc)

    def interp(n, _):
        wait_bytes(arrived.at[n, others], ar_sem.at[n])
        w = weight_ref[pl.ds(pl.multiple_of(n * LANES, LANES), LANES), :]
        u_acc[...] += jnp.dot(arrived[n, :, 0:LANES], w, preferred_element_type=f32)
        v_acc[...] += jnp.dot(arrived[n, :, LANES:width], w, preferred_element_type=f32)
        return 0

    lax.fori_loop(0, chunks, interp, 0)
    wait_bytes(o_recv.at[pl.ds(0, blk - 1)], or_sem)
    per = LANES // cap
    pieces = []
    for g in range(blk // per):
        total = o_recv[g * per]
        for j in range(1, per):
            total = total + o_recv[g * per + j]
        pieces.append(total)
    total = jnp.zeros((MAPH, columns), f32)
    for g in range(slots // LANES):
        cut = slice(g * LANES, (g + 1) * LANES)
        spot = iota((MAPH, LANES), 0) == pieces[g].astype(jnp.int32) - 1
        spot = spot.astype(f32).astype(bf16)
        u, v = u_acc[cut, :], v_acc[cut, :]
        power = u * u + v * v
        high = power.astype(bf16)
        rest = power - high.astype(f32)
        mid = rest.astype(bf16)
        low = (rest - mid.astype(f32)).astype(bf16)
        for part in (high, mid, low):
            total = total + jnp.dot(spot, part, preferred_element_type=f32)
    out_ref[...] = total

    for sem in range(7):
        wait_bytes(blocks.at[0], g_send.at[sem])
    for n in range(chunks):
        wait_bytes(x_send.at[n], xs_sem.at[n])
        wait_bytes(packed.at[n, others], as_sem.at[n])
    wait_bytes(o_send.at[pl.ds(0, blk - 1)], os_sem)


def body(phase_history, tile_curvature, interp_weights, strip_tiles, row_offsets, tile_owner):
    blk = lax.axis_size("blk")
    maps = lax.axis_size("map")
    pulses = phase_history.shape[2]
    freqs = phase_history.shape[3] // 2
    columns = interp_weights.shape[2]
    rows = strip_tiles.shape[2]
    cap = max(TILE, 2 * rows // blk)
    slots = blk * cap
    chunks = columns // LANES
    width = 2 * LANES
    stacked = STOPS * pulses
    f32, bf16 = jnp.float32, jnp.bfloat16
    vmem = pl.BlockSpec(memory_space=pltpu.VMEM)
    dma = pltpu.SemaphoreType.DMA
    out = pl.pallas_call(
        functools.partial(kernel, (blk, maps, pulses, freqs, columns, rows, cap)),
        out_shape=jax.ShapeDtypeStruct((MAPH, columns), f32),
        in_specs=[vmem, pl.BlockSpec(memory_space=pltpu.SMEM), vmem, vmem, vmem, vmem],
        out_specs=vmem,
        scratch_shapes=[
            pltpu.VMEM((STOPS, pulses, 2 * freqs), bf16),
            pltpu.VMEM((chunks, 2 * freqs, width), bf16),
            pltpu.VMEM((rows * maps, 2 * stacked), bf16),
            pltpu.VMEM((pulses, 2 * freqs), bf16),
            pltpu.VMEM((chunks, 2 * stacked, width), bf16),
            pltpu.VMEM((chunks, rows, width), bf16),
            pltpu.VMEM((chunks, rows, width), bf16),
            pltpu.VMEM((chunks, rows, width), f32),
            pltpu.VMEM((chunks, slots, width), bf16),
            pltpu.VMEM((chunks, slots, width), bf16),
            pltpu.VMEM((slots, rows), bf16),
            pltpu.VMEM((blk, 1, LANES), f32),
            pltpu.VMEM((blk, 1, LANES), f32),
            pltpu.VMEM((slots, columns), f32),
            pltpu.VMEM((slots, columns), f32),
            dma((7,)), dma((STOPS,)), dma((chunks,)), dma((chunks,)),
            dma((chunks,)), dma((chunks,)), dma, dma,
        ],
        compiler_params=pltpu.CompilerParams(
            collective_id=0, has_side_effects=True, vmem_limit_bytes=60 * 2**20),
    )(
        phase_history[0, 0], tile_curvature, interp_weights[0],
        strip_tiles[0, 0].reshape(1, rows), row_offsets[0],
        tile_owner.reshape(blk, 1),
    )
    return out.reshape(1, 1, MAPH, columns)


def solution(mesh):
    in_specs = (
        P("blk", "map", None, None),
        P("blk"),
        P("blk", None, None),
        P("blk", "map", None, None),
        P("blk", "map", None),
        P(),
    )
    out_specs = P("blk", "map", None, None)
    return jax.shard_map(body, mesh=mesh, in_specs=in_specs, out_specs=out_specs, check_vma=False)
```

```python
import functools
import math

import jax
import jax.numpy as jnp
import numpy as np
from jax import lax
from jax.experimental import pallas as pl
from jax.experimental.pallas import tpu as pltpu
from jax.sharding import PartitionSpec as P

STOPS = 8
MAPH = 256
LANES = 128
TILE = 16


def fit_turns():
    z = 0.125 - 0.125 * np.cos(np.pi * (np.arange(400) + 0.5) / 400)
    t = np.sqrt(z)
    cheb = np.polynomial.chebyshev.Chebyshev
    cos_fit = cheb.fit(z, np.cos(2 * np.pi * t), 7, domain=[0, 0.25])
    sin_fit = cheb.fit(z, np.sin(2 * np.pi * t) / t, 6, domain=[0, 0.25])
    power = np.polynomial.Polynomial
    return (
        [float(np.float32(c)) for c in cos_fit.convert(kind=power).coef],
        [float(np.float32(c)) for c in sin_fit.convert(kind=power).coef],
    )


COS_COEF, SIN_COEF = fit_turns()


def cos_sin_turns(turns):
    t = turns - jnp.round(turns)
    z = t * t
    c = jnp.full_like(z, COS_COEF[-1])
    for coef in COS_COEF[-2::-1]:
        c = c * z + coef
    s = jnp.full_like(z, SIN_COEF[-1])
    for coef in SIN_COEF[-2::-1]:
        s = s * z + coef
    return c, s * t


def iota(shape, axis):
    return lax.broadcasted_iota(jnp.int32, shape, axis)


def kernel(
    sizes,
    block_ref, curv_ref, weight_ref, tiles_ref, offs_ref, owner_ref,
    out_ref,
    blocks, ranges, cross, phased, right, weights, x_send, x_recv, x_own, packed, arrived, slot_hot,
    o_send, o_recv, u_acc, v_acc,
    g_send, g_recv, xs_sem, xr_sem, as_sem, ar_sem, os_sem, or_sem,
):
    blk, maps, pulses, freqs, columns, rows, cap = sizes
    f32, bf16 = jnp.float32, jnp.bfloat16
    me = lax.axis_index("blk")
    my_map = lax.axis_index("map")
    other_map = 1 - my_map
    core = lax.rem(me, 2)
    span = STOPS * maps * pulses
    stacked = STOPS // 2 * pulses
    chunks = columns // LANES
    width = 2 * LANES
    slots = blk * cap
    own_stop = STOPS // 2 - 1

    def device(index):
        return (lax.rem(index + 2 * blk, blk), my_map)

    mesh_id = pl.DeviceIdType.MESH

    barrier = pltpu.get_barrier_semaphore()

    def greet(i, _):
        pl.semaphore_signal(barrier, inc=1, device_id=device(me + i), device_id_type=mesh_id)
        return 0

    lax.fori_loop(1, blk, greet, 0)
    pl.semaphore_signal(barrier, inc=1, device_id=(me, other_map), device_id_type=mesh_id)
    blocks[own_stop] = block_ref[...]
    pl.semaphore_wait(barrier, blk)

    def push(source, stop, target, sem):
        return pltpu.make_async_remote_copy(
            src_ref=source, dst_ref=blocks.at[stop], send_sem=g_send.at[sem],
            recv_sem=g_recv.at[stop], device_id=target, device_id_type=mesh_id)

    def arrived_block(stop):
        pltpu.make_async_copy(blocks.at[stop], blocks.at[stop], g_recv.at[stop]).wait()

    partner = device(me + 1 - 2 * core)
    shift = 2 * core - 1

    push(block_ref, 7, device(me - 4), 0).start()

    @pl.when(core == 1)
    def _():
        push(block_ref, 0, device(me + 3), 6).start()

    push(block_ref, 5, device(me - 2), 1).start()
    push(block_ref, 1, device(me + 2), 2).start()
    push(block_ref, own_stop + shift, partner, 3).start()

    half_freqs = freqs // 2
    half_chunks = chunks // 2
    half_rows = rows // 2

    def fill_ranges(i, _):
        at = pl.ds(pl.multiple_of(i * TILE, TILE), TILE)
        below = pl.ds(pl.multiple_of(half_freqs + i * TILE, TILE), TILE)
        f = (i * TILE + iota((TILE, columns // 2), 0)).astype(f32)
        for odd in range(2):
            c = (2 * iota((TILE, columns // 2), 1) + odd).astype(f32)
            re, im = cos_sin_turns(f * c * (1.0 / freqs))
            re = (re * (1.0 / math.sqrt(freqs))).astype(bf16)
            im = (im * (1.0 / math.sqrt(freqs)))
            pos, neg = im.astype(bf16), (-im).astype(bf16)
            for n in range(half_chunks):
                cut = slice(n * LANES, (n + 1) * LANES)
                left = slice(n * width, n * width + LANES)
                rest = slice(n * width + LANES, (n + 1) * width)
                ranges[odd, at, left] = re[:, cut]
                ranges[odd, at, rest] = neg[:, cut]
                ranges[odd, below, left] = pos[:, cut]
                ranges[odd, below, rest] = re[:, cut]
        return 0

    lax.fori_loop(0, half_freqs // TILE, fill_ranges, 0)

    lane = iota((1, stacked), 1)
    q_lane = (lane + (lax.div(lane, pulses) * (maps - 1) + my_map) * pulses).astype(f32)

    def fill_cross(i, _):
        at = pl.ds(pl.multiple_of(i * TILE, TILE), TILE)
        g = i * TILE
        odd = lax.div(g, rows)
        own = lax.div(lax.rem(g, rows), half_rows)
        part = jnp.where(own == 1, my_map, other_map)
        base = part * rows + odd + 2 * lax.rem(g, half_rows)
        a = (base + 2 * iota((TILE, stacked), 0)).astype(f32)
        re, im = cos_sin_turns(a * q_lane * (1.0 / span))
        cross[at, 0:stacked] = (re * (1.0 / math.sqrt(span))).astype(bf16)
        cross[at, stacked:2 * stacked] = (im * (-1.0 / math.sqrt(span))).astype(bf16)
        return 0

    lax.fori_loop(0, rows * maps // TILE, fill_cross, 0)

    def fill_slots():
        tiles = tiles_ref[...]
        holders = iota((blk, rows), 0)
        dest = jnp.sum(jnp.where(holders == tiles, owner_ref[...], 0), axis=0, keepdims=True)
        hot = (holders == dest).astype(f32)
        upto = (iota((rows, rows), 0) <= iota((rows, rows), 1)).astype(f32).astype(bf16)
        counts = jnp.dot(hot.astype(bf16), upto, preferred_element_type=f32)
        rank = jnp.sum(counts * hot, axis=0, keepdims=True).astype(jnp.int32) - 1
        slot = dest * cap + rank
        spot = iota((rows, rows), 1)
        spot = 2 * lax.rem(spot, half_rows) + lax.div(spot, half_rows)
        order = (iota((rows, rows), 0) == spot).astype(f32).astype(bf16)
        for i in range(slots // LANES):
            at = i * LANES + iota((LANES, rows), 0)
            hits = (at == slot).astype(f32).astype(bf16)
            slot_hot[i * LANES:(i + 1) * LANES, :] = jnp.dot(
                hits, order, preferred_element_type=f32).astype(bf16)
        place = lax.rem(me, LANES // cap) * cap + rank
        marks = jnp.where(iota((LANES, rows), 0) == place, (offs_ref[...] + 1).astype(f32), 0.0)
        table = lax.dot_general(
            hot.astype(bf16), marks.astype(bf16), (((1,), (1,)), ((), ())),
            preferred_element_type=f32)
        for d in range(blk):
            o_send[d] = table[d:d + 1, :]
        o_recv[me] = o_send[me]

        def send(i, _):
            to = lax.rem(me + i, blk)
            pltpu.make_async_remote_copy(
                src_ref=o_send.at[to], dst_ref=o_recv.at[me], send_sem=os_sem,
                recv_sem=or_sem, device_id=(to, my_map), device_id_type=mesh_id).start()
            return 0

        lax.fori_loop(1, blk, send, 0)

    fill_slots()

    def order_weights(i, _):
        at = pl.ds(pl.multiple_of(i * LANES, LANES), LANES)
        r = i * LANES + iota((LANES, columns), 0)
        r = 2 * lax.rem(r, columns // 2) + lax.div(r, columns // 2)
        order = (iota((LANES, columns), 1) == r).astype(f32).astype(bf16)
        weights[at, :] = jnp.dot(
            order, weight_ref[...], preferred_element_type=f32).astype(bf16)
        return 0

    lax.fori_loop(0, chunks, order_weights, 0)

    curvature = curv_ref[0]

    def turned(k, i):
        at = pl.ds(pl.multiple_of(i * TILE, TILE), TILE)
        q = (k * maps + my_map) * pulses + i * TILE + iota((TILE, freqs), 0)
        s = q.astype(f32) * (1.0 / span) - 0.5
        r = iota((TILE, freqs), 1).astype(f32) * (1.0 / freqs) - 0.5
        angle = curvature * (s * s) * (1.0 + r)
        c, si = cos_sin_turns(angle * (0.5 / math.pi))
        re = blocks[k, at, 0:freqs].astype(f32)
        im = blocks[k, at, freqs:2 * freqs].astype(f32)
        return re * c - im * si, re * si + im * c

    def spectrum(j):
        def turn(i, _):
            first = turned(j, i)
            second = turned(j + STOPS // 2, i)
            for part in range(2):
                z_sum, z_diff = first[part] + second[part], first[part] - second[part]
                to = slice(part * half_freqs, (part + 1) * half_freqs)
                for odd_row, z in ((0, z_sum), (1, z_diff)):
                    at = pl.ds(pl.multiple_of(odd_row * pulses + i * TILE, TILE), TILE)
                    near, far = z[:, :half_freqs], z[:, half_freqs:]
                    phased[0, at, to] = (near + far).astype(bf16)
                    phased[1, at, to] = (near - far).astype(bf16)
            return 0

        lax.fori_loop(0, pulses // TILE, turn, 0)
        top = pl.ds(pl.multiple_of(j * pulses, pulses), pulses)
        low = pl.ds(pl.multiple_of(stacked + j * pulses, pulses), pulses)

        def columns_of(odd, _):
            y = jnp.dot(phased[odd], ranges[odd], preferred_element_type=f32)
            for h in range(half_chunks):
                n = odd * half_chunks + h
                yr = y[:, h * width:h * width + LANES]
                yi = y[:, h * width + LANES:(h + 1) * width]
                for odd_row in range(2):
                    cut = slice(odd_row * pulses, (odd_row + 1) * pulses)
                    real, imag = yr[cut].astype(bf16), yi[cut].astype(bf16)
                    right[n, odd_row, top, 0:LANES] = real
                    right[n, odd_row, top, LANES:width] = imag
                    right[n, odd_row, low, 0:LANES] = (-yi[cut]).astype(bf16)
                    right[n, odd_row, low, LANES:width] = real
            return 0

        lax.fori_loop(0, 2, columns_of, 0)

    def step(i, _):
        j = jnp.where(i == 0, 1, jnp.where(i == 1, 3, jnp.where(i == 2, 0, 2)))

        @pl.when(i == 0)
        def _():
            arrived_block(5)
            push(blocks.at[5], 5 + shift, partner, 4).start()
            arrived_block(1)
            push(blocks.at[1], 1 + shift, partner, 5).start()

        @pl.when(i == 1)
        def _():
            arrived_block(7)

            @pl.when(core == 0)
            def _():
                push(blocks.at[7], 6, partner, 6).start()

        @pl.when(i >= 2)
        def _():
            arrived_block(j)
            arrived_block(j + STOPS // 2)

        spectrum(j)
        return 0

    lax.fori_loop(0, STOPS // 2, step, 0)

    def x_copy(n):
        return pltpu.make_async_remote_copy(
            src_ref=x_send.at[n], dst_ref=x_recv.at[n], send_sem=xs_sem.at[n],
            recv_sem=xr_sem.at[n], device_id=(me, other_map), device_id_type=mesh_id)

    own_slots = pl.ds(pl.multiple_of(me * cap, cap), cap)

    def column_step(n, _):
        @pl.when(n < chunks)
        def _():
            for odd_row in range(2):
                table = cross[odd_row * rows:(odd_row + 1) * rows, :]
                y = jnp.dot(table, right[n, odd_row], preferred_element_type=f32)
                to = slice(odd_row * half_rows, (odd_row + 1) * half_rows)
                x_send[n, to, :] = y[:half_rows].astype(bf16)
                x_own[n, to, :] = y[half_rows:]
            x_copy(n).start()

        @pl.when(n >= 1)
        def _():
            b = n - 1
            x_copy(b).wait_recv()
            image = (x_own[b] + x_recv[b].astype(f32)).astype(bf16)
            packed[b] = jnp.dot(slot_hot[...], image, preferred_element_type=f32).astype(bf16)

            def send(i, _):
                to = lax.rem(me + i, blk)
                pltpu.make_async_remote_copy(
                    src_ref=packed.at[b, pl.ds(pl.multiple_of(to * cap, cap), cap)],
                    dst_ref=arrived.at[b, own_slots], send_sem=as_sem.at[b],
                    recv_sem=ar_sem.at[b], device_id=(to, my_map),
                    device_id_type=mesh_id).start()
                return 0

            lax.fori_loop(1, blk, send, 0)
            arrived[b, own_slots, :] = packed[b, own_slots, :]

        return 0

    lax.fori_loop(0, chunks + 1, column_step, 0)

    def wait_bytes(ref, sem):
        pltpu.make_async_copy(ref, ref, sem).wait()

    others = pl.ds(0, (blk - 1) * cap)
    u_acc[...] = jnp.zeros_like(u_acc)
    v_acc[...] = jnp.zeros_like(v_acc)

    def interp(n, _):
        wait_bytes(arrived.at[n, others], ar_sem.at[n])
        w = weights[pl.ds(pl.multiple_of(n * LANES, LANES), LANES), :]
        u_acc[...] += jnp.dot(arrived[n, :, 0:LANES], w, preferred_element_type=f32)
        v_acc[...] += jnp.dot(arrived[n, :, LANES:width], w, preferred_element_type=f32)
        return 0

    lax.fori_loop(0, chunks, interp, 0)
    wait_bytes(o_recv.at[pl.ds(0, blk - 1)], or_sem)
    per = LANES // cap
    pieces = []
    for g in range(blk // per):
        total = o_recv[g * per]
        for j in range(1, per):
            total = total + o_recv[g * per + j]
        pieces.append(total)
    total = jnp.zeros((MAPH, columns), f32)
    for g in range(slots // LANES):
        cut = slice(g * LANES, (g + 1) * LANES)
        spot = iota((MAPH, LANES), 0) == pieces[g].astype(jnp.int32) - 1
        spot = spot.astype(f32).astype(bf16)
        u, v = u_acc[cut, :], v_acc[cut, :]
        power = u * u + v * v
        high = power.astype(bf16)
        rest = power - high.astype(f32)
        mid = rest.astype(bf16)
        low = (rest - mid.astype(f32)).astype(bf16)
        for part in (high, mid, low):
            total = total + jnp.dot(spot, part, preferred_element_type=f32)
    out_ref[...] = total

    for sem in range(7):
        wait_bytes(blocks.at[0], g_send.at[sem])
    for n in range(chunks):
        wait_bytes(x_send.at[n], xs_sem.at[n])
        wait_bytes(packed.at[n, others], as_sem.at[n])
    wait_bytes(o_send.at[pl.ds(0, blk - 1)], os_sem)


def body(phase_history, tile_curvature, interp_weights, strip_tiles, row_offsets, tile_owner):
    blk = lax.axis_size("blk")
    maps = lax.axis_size("map")
    pulses = phase_history.shape[2]
    freqs = phase_history.shape[3] // 2
    columns = interp_weights.shape[2]
    rows = strip_tiles.shape[2]
    cap = max(TILE, 2 * rows // blk)
    slots = blk * cap
    chunks = columns // LANES
    width = 2 * LANES
    stacked = STOPS // 2 * pulses
    f32, bf16 = jnp.float32, jnp.bfloat16
    vmem = pl.BlockSpec(memory_space=pltpu.VMEM)
    dma = pltpu.SemaphoreType.DMA
    out = pl.pallas_call(
        functools.partial(kernel, (blk, maps, pulses, freqs, columns, rows, cap)),
        out_shape=jax.ShapeDtypeStruct((MAPH, columns), f32),
        in_specs=[vmem, pl.BlockSpec(memory_space=pltpu.SMEM), vmem, vmem, vmem, vmem],
        out_specs=vmem,
        scratch_shapes=[
            pltpu.VMEM((STOPS, pulses, 2 * freqs), bf16),
            pltpu.VMEM((2, freqs, columns), bf16),
            pltpu.VMEM((rows * maps, 2 * stacked), bf16),
            pltpu.VMEM((2, 2 * pulses, freqs), bf16),
            pltpu.VMEM((chunks, 2, 2 * stacked, width), bf16),
            pltpu.VMEM((columns, columns), bf16),
            pltpu.VMEM((chunks, rows, width), bf16),
            pltpu.VMEM((chunks, rows, width), bf16),
            pltpu.VMEM((chunks, rows, width), f32),
            pltpu.VMEM((chunks, slots, width), bf16),
            pltpu.VMEM((chunks, slots, width), bf16),
            pltpu.VMEM((slots, rows), bf16),
            pltpu.VMEM((blk, 1, LANES), f32),
            pltpu.VMEM((blk, 1, LANES), f32),
            pltpu.VMEM((slots, columns), f32),
            pltpu.VMEM((slots, columns), f32),
            dma((7,)), dma((STOPS,)), dma((chunks,)), dma((chunks,)),
            dma((chunks,)), dma((chunks,)), dma, dma,
        ],
        compiler_params=pltpu.CompilerParams(
            collective_id=0, has_side_effects=True, vmem_limit_bytes=60 * 2**20),
    )(
        phase_history[0, 0], tile_curvature, interp_weights[0],
        strip_tiles[0, 0].reshape(1, rows), row_offsets[0],
        tile_owner.reshape(blk, 1),
    )
    return out.reshape(1, 1, MAPH, columns)


def solution(mesh):
    in_specs = (
        P("blk", "map", None, None),
        P("blk"),
        P("blk", None, None),
        P("blk", "map", None, None),
        P("blk", "map", None),
        P(),
    )
    out_specs = P("blk", "map", None, None)
    return jax.shard_map(body, mesh=mesh, in_specs=in_specs, out_specs=out_specs, check_vma=False)
```

```python
import functools
import math

import jax
import jax.numpy as jnp
import numpy as np
from jax import lax
from jax.experimental import pallas as pl
from jax.experimental.pallas import tpu as pltpu
from jax.sharding import PartitionSpec as P

STOPS = 8
MAPH = 256
LANES = 128
TILE = 16


def fit_turns():
    z = 0.125 - 0.125 * np.cos(np.pi * (np.arange(400) + 0.5) / 400)
    t = np.sqrt(z)
    cheb = np.polynomial.chebyshev.Chebyshev
    cos_fit = cheb.fit(z, np.cos(2 * np.pi * t), 7, domain=[0, 0.25])
    sin_fit = cheb.fit(z, np.sin(2 * np.pi * t) / t, 6, domain=[0, 0.25])
    power = np.polynomial.Polynomial
    return (
        [float(np.float32(c)) for c in cos_fit.convert(kind=power).coef],
        [float(np.float32(c)) for c in sin_fit.convert(kind=power).coef],
    )


COS_COEF, SIN_COEF = fit_turns()


def cos_sin_turns(turns):
    t = turns - jnp.round(turns)
    z = t * t
    c = jnp.full_like(z, COS_COEF[-1])
    for coef in COS_COEF[-2::-1]:
        c = c * z + coef
    s = jnp.full_like(z, SIN_COEF[-1])
    for coef in SIN_COEF[-2::-1]:
        s = s * z + coef
    return c, s * t


def iota(shape, axis):
    return lax.broadcasted_iota(jnp.int32, shape, axis)


def kernel(
    sizes,
    block_ref, curv_ref, weight_ref, tiles_ref, offs_ref, owner_ref,
    out_ref,
    blocks, ranges, cross, phased, right, weights, x_send, x_recv, x_own, packed, arrived, slot_hot,
    o_send, o_recv, u_acc, v_acc,
    g_send, g_recv, xs_sem, xr_sem, as_sem, ar_sem, os_sem, or_sem,
):
    blk, maps, pulses, freqs, columns, rows, cap = sizes
    f32, bf16 = jnp.float32, jnp.bfloat16
    me = lax.axis_index("blk")
    my_map = lax.axis_index("map")
    other_map = 1 - my_map
    core = lax.rem(me, 2)
    span = STOPS * maps * pulses
    stacked = STOPS // 2 * pulses
    chunks = columns // LANES
    width = 2 * LANES
    slots = blk * cap
    own_stop = STOPS // 2 - 1

    def device(index):
        return (lax.rem(index + 2 * blk, blk), my_map)

    mesh_id = pl.DeviceIdType.MESH

    barrier = pltpu.get_barrier_semaphore()

    def greet(i, _):
        pl.semaphore_signal(barrier, inc=1, device_id=device(me + i), device_id_type=mesh_id)
        return 0

    lax.fori_loop(1, blk, greet, 0)
    pl.semaphore_signal(barrier, inc=1, device_id=(me, other_map), device_id_type=mesh_id)
    blocks[own_stop] = block_ref[...]
    pl.semaphore_wait(barrier, blk)

    def push(source, stop, target, sem):
        return pltpu.make_async_remote_copy(
            src_ref=source, dst_ref=blocks.at[stop], send_sem=g_send.at[sem],
            recv_sem=g_recv.at[stop], device_id=target, device_id_type=mesh_id)

    def arrived_block(stop):
        pltpu.make_async_copy(blocks.at[stop], blocks.at[stop], g_recv.at[stop]).wait()

    partner = device(me + 1 - 2 * core)
    shift = 2 * core - 1

    push(block_ref, 7, device(me - 4), 0).start()

    @pl.when(core == 1)
    def _():
        push(block_ref, 0, device(me + 3), 6).start()

    push(block_ref, 5, device(me - 2), 1).start()
    push(block_ref, 1, device(me + 2), 2).start()
    push(block_ref, own_stop + shift, partner, 3).start()

    half_freqs = freqs // 2
    half_chunks = chunks // 2
    half_rows = rows // 2

    def fill_ranges(i, _):
        at = pl.ds(pl.multiple_of(i * TILE, TILE), TILE)
        below = pl.ds(pl.multiple_of(half_freqs + i * TILE, TILE), TILE)
        f = (i * TILE + iota((TILE, columns // 2), 0)).astype(f32)
        for odd in range(2):
            c = (2 * iota((TILE, columns // 2), 1) + odd).astype(f32)
            re, im = cos_sin_turns(f * c * (1.0 / freqs))
            re = (re * (1.0 / math.sqrt(freqs))).astype(bf16)
            im = (im * (1.0 / math.sqrt(freqs)))
            pos, neg = im.astype(bf16), (-im).astype(bf16)
            for n in range(half_chunks):
                cut = slice(n * LANES, (n + 1) * LANES)
                to = odd * half_chunks + n
                ranges[to, at, 0:LANES] = re[:, cut]
                ranges[to, at, LANES:width] = neg[:, cut]
                ranges[to, below, 0:LANES] = pos[:, cut]
                ranges[to, below, LANES:width] = re[:, cut]
        return 0

    lax.fori_loop(0, half_freqs // TILE, fill_ranges, 0)

    lane = iota((1, stacked), 1)
    q_lane = (lane + (lax.div(lane, pulses) * (maps - 1) + my_map) * pulses).astype(f32)

    def fill_cross(i, _):
        at = pl.ds(pl.multiple_of(i * TILE, TILE), TILE)
        g = i * TILE
        odd = lax.div(g, rows)
        own = lax.div(lax.rem(g, rows), half_rows)
        part = jnp.where(own == 1, my_map, other_map)
        base = part * rows + odd + 2 * lax.rem(g, half_rows)
        a = (base + 2 * iota((TILE, stacked), 0)).astype(f32)
        re, im = cos_sin_turns(a * q_lane * (1.0 / span))
        cross[at, 0:stacked] = (re * (1.0 / math.sqrt(span))).astype(bf16)
        cross[at, stacked:2 * stacked] = (im * (-1.0 / math.sqrt(span))).astype(bf16)
        return 0

    lax.fori_loop(0, rows * maps // TILE, fill_cross, 0)

    def fill_slots():
        tiles = tiles_ref[...]
        holders = iota((blk, rows), 0)
        named = (holders == tiles).astype(f32).astype(bf16)
        holds = (iota((blk, blk), 0) == owner_ref[...]).astype(f32).astype(bf16)
        hot = jnp.dot(holds, named, preferred_element_type=f32)
        dest = jnp.sum(holders.astype(f32) * hot, axis=0, keepdims=True).astype(jnp.int32)
        upto = (iota((rows, rows), 0) <= iota((rows, rows), 1)).astype(f32).astype(bf16)
        counts = jnp.dot(hot.astype(bf16), upto, preferred_element_type=f32)
        rank = jnp.sum(counts * hot, axis=0, keepdims=True).astype(jnp.int32) - 1
        slot = dest * cap + rank
        spot = iota((rows, rows), 1)
        spot = 2 * lax.rem(spot, half_rows) + lax.div(spot, half_rows)
        order = (iota((rows, rows), 0) == spot).astype(f32).astype(bf16)
        for i in range(slots // LANES):
            at = i * LANES + iota((LANES, rows), 0)
            hits = (at == slot).astype(f32).astype(bf16)
            slot_hot[i * LANES:(i + 1) * LANES, :] = jnp.dot(
                hits, order, preferred_element_type=f32).astype(bf16)
        place = lax.rem(me, LANES // cap) * cap + rank
        marks = jnp.where(iota((LANES, rows), 0) == place, (offs_ref[...] + 1).astype(f32), 0.0)
        table = lax.dot_general(
            hot.astype(bf16), marks.astype(bf16), (((1,), (1,)), ((), ())),
            preferred_element_type=f32)
        for d in range(blk):
            o_send[d] = table[d:d + 1, :]
        o_recv[me] = o_send[me]

        def send(i, _):
            to = lax.rem(me + i, blk)
            pltpu.make_async_remote_copy(
                src_ref=o_send.at[to], dst_ref=o_recv.at[me], send_sem=os_sem,
                recv_sem=or_sem, device_id=(to, my_map), device_id_type=mesh_id).start()
            return 0

        lax.fori_loop(1, blk, send, 0)

    fill_slots()

    def order_weights(i, _):
        at = pl.ds(pl.multiple_of(i * LANES, LANES), LANES)
        r = i * LANES + iota((LANES, columns), 0)
        r = 2 * lax.rem(r, columns // 2) + lax.div(r, columns // 2)
        order = (iota((LANES, columns), 1) == r).astype(f32).astype(bf16)
        weights[at, :] = jnp.dot(
            order, weight_ref[...], preferred_element_type=f32).astype(bf16)
        return 0

    lax.fori_loop(0, chunks, order_weights, 0)

    curvature = curv_ref[0]

    def turned(k, i):
        at = pl.ds(pl.multiple_of(i * TILE, TILE), TILE)
        q = (k * maps + my_map) * pulses + i * TILE + iota((TILE, freqs), 0)
        s = q.astype(f32) * (1.0 / span) - 0.5
        r = iota((TILE, freqs), 1).astype(f32) * (1.0 / freqs) - 0.5
        angle = curvature * (s * s) * (1.0 + r)
        c, si = cos_sin_turns(angle * (0.5 / math.pi))
        re = blocks[k, at, 0:freqs].astype(f32)
        im = blocks[k, at, freqs:2 * freqs].astype(f32)
        return re * c - im * si, re * si + im * c

    def spectrum(j):
        def turn(i, _):
            first = turned(j, i)
            second = turned(j + STOPS // 2, i)
            for part in range(2):
                z_sum, z_diff = first[part] + second[part], first[part] - second[part]
                to = slice(part * half_freqs, (part + 1) * half_freqs)
                for odd_row, z in ((0, z_sum), (1, z_diff)):
                    at = pl.ds(pl.multiple_of(odd_row * pulses + i * TILE, TILE), TILE)
                    near, far = z[:, :half_freqs], z[:, half_freqs:]
                    phased[0, at, to] = (near + far).astype(bf16)
                    phased[1, at, to] = (near - far).astype(bf16)
            return 0

        lax.fori_loop(0, pulses // TILE, turn, 0, unroll=2)
        top = pl.ds(pl.multiple_of(j * pulses, pulses), pulses)
        low = pl.ds(pl.multiple_of(stacked + j * pulses, pulses), pulses)

        def columns_of(n, _):
            odd = lax.div(n, half_chunks)
            y = jnp.dot(phased[odd], ranges[n], preferred_element_type=f32)
            yr, yi = y[:, :LANES], y[:, LANES:]
            for odd_row in range(2):
                cut = slice(odd_row * pulses, (odd_row + 1) * pulses)
                real, imag = yr[cut].astype(bf16), yi[cut].astype(bf16)
                right[n, odd_row, top, 0:LANES] = real
                right[n, odd_row, top, LANES:width] = imag
                right[n, odd_row, low, 0:LANES] = (-yi[cut]).astype(bf16)
                right[n, odd_row, low, LANES:width] = real
            return 0

        lax.fori_loop(0, chunks, columns_of, 0, unroll=True)

    def step(i, _):
        j = jnp.where(i == 0, 1, jnp.where(i == 1, 3, jnp.where(i == 2, 0, 2)))

        @pl.when(i == 0)
        def _():
            arrived_block(5)
            push(blocks.at[5], 5 + shift, partner, 4).start()
            arrived_block(1)
            push(blocks.at[1], 1 + shift, partner, 5).start()

        @pl.when(i == 1)
        def _():
            arrived_block(7)

            @pl.when(core == 0)
            def _():
                push(blocks.at[7], 6, partner, 6).start()

        @pl.when(i >= 2)
        def _():
            arrived_block(j)
            arrived_block(j + STOPS // 2)

        spectrum(j)
        return 0

    lax.fori_loop(0, STOPS // 2, step, 0)

    def x_copy(n):
        return pltpu.make_async_remote_copy(
            src_ref=x_send.at[n], dst_ref=x_recv.at[n], send_sem=xs_sem.at[n],
            recv_sem=xr_sem.at[n], device_id=(me, other_map), device_id_type=mesh_id)

    own_slots = pl.ds(pl.multiple_of(me * cap, cap), cap)

    def column_step(n, _):
        @pl.when(n < chunks)
        def _():
            for odd_row in range(2):
                table = cross[odd_row * rows:(odd_row + 1) * rows, :]
                y = jnp.dot(table, right[n, odd_row], preferred_element_type=f32)
                to = slice(odd_row * half_rows, (odd_row + 1) * half_rows)
                x_send[n, to, :] = y[:half_rows].astype(bf16)
                x_own[n, to, :] = y[half_rows:]
            x_copy(n).start()

        @pl.when(n >= 1)
        def _():
            b = n - 1
            x_copy(b).wait_recv()
            image = (x_own[b] + x_recv[b].astype(f32)).astype(bf16)
            packed[b] = jnp.dot(slot_hot[...], image, preferred_element_type=f32).astype(bf16)

            def send(i, _):
                to = lax.rem(me + i, blk)
                pltpu.make_async_remote_copy(
                    src_ref=packed.at[b, pl.ds(pl.multiple_of(to * cap, cap), cap)],
                    dst_ref=arrived.at[b, own_slots], send_sem=as_sem.at[b],
                    recv_sem=ar_sem.at[b], device_id=(to, my_map),
                    device_id_type=mesh_id).start()
                return 0

            lax.fori_loop(1, blk, send, 0)
            arrived[b, own_slots, :] = packed[b, own_slots, :]

        return 0

    lax.fori_loop(0, chunks + 1, column_step, 0)

    def wait_bytes(ref, sem):
        pltpu.make_async_copy(ref, ref, sem).wait()

    others = pl.ds(0, (blk - 1) * cap)
    u_acc[...] = jnp.zeros_like(u_acc)
    v_acc[...] = jnp.zeros_like(v_acc)

    def interp(n, _):
        wait_bytes(arrived.at[n, others], ar_sem.at[n])
        w = weights[pl.ds(pl.multiple_of(n * LANES, LANES), LANES), :]
        u_acc[...] += jnp.dot(arrived[n, :, 0:LANES], w, preferred_element_type=f32)
        v_acc[...] += jnp.dot(arrived[n, :, LANES:width], w, preferred_element_type=f32)
        return 0

    lax.fori_loop(0, chunks, interp, 0, unroll=True)
    wait_bytes(o_recv.at[pl.ds(0, blk - 1)], or_sem)
    per = LANES // cap
    pieces = []
    for g in range(blk // per):
        total = o_recv[g * per]
        for j in range(1, per):
            total = total + o_recv[g * per + j]
        pieces.append(total)
    total = jnp.zeros((MAPH, columns), f32)
    for g in range(slots // LANES):
        cut = slice(g * LANES, (g + 1) * LANES)
        spot = iota((MAPH, LANES), 0) == pieces[g].astype(jnp.int32) - 1
        spot = spot.astype(f32).astype(bf16)
        u, v = u_acc[cut, :], v_acc[cut, :]
        power = u * u + v * v
        high = power.astype(bf16)
        rest = power - high.astype(f32)
        mid = rest.astype(bf16)
        low = (rest - mid.astype(f32)).astype(bf16)
        for part in (high, mid, low):
            total = total + jnp.dot(spot, part, preferred_element_type=f32)
    out_ref[...] = total

    for sem in range(7):
        wait_bytes(blocks.at[0], g_send.at[sem])
    for n in range(chunks):
        wait_bytes(x_send.at[n], xs_sem.at[n])
        wait_bytes(packed.at[n, others], as_sem.at[n])
    wait_bytes(o_send.at[pl.ds(0, blk - 1)], os_sem)


def body(phase_history, tile_curvature, interp_weights, strip_tiles, row_offsets, tile_owner):
    blk = lax.axis_size("blk")
    maps = lax.axis_size("map")
    pulses = phase_history.shape[2]
    freqs = phase_history.shape[3] // 2
    columns = interp_weights.shape[2]
    rows = strip_tiles.shape[2]
    cap = max(TILE, 2 * rows // blk)
    slots = blk * cap
    chunks = columns // LANES
    width = 2 * LANES
    stacked = STOPS // 2 * pulses
    f32, bf16 = jnp.float32, jnp.bfloat16
    vmem = pl.BlockSpec(memory_space=pltpu.VMEM)
    dma = pltpu.SemaphoreType.DMA
    out = pl.pallas_call(
        functools.partial(kernel, (blk, maps, pulses, freqs, columns, rows, cap)),
        out_shape=jax.ShapeDtypeStruct((MAPH, columns), f32),
        in_specs=[vmem, pl.BlockSpec(memory_space=pltpu.SMEM), vmem, vmem, vmem, vmem],
        out_specs=vmem,
        scratch_shapes=[
            pltpu.VMEM((STOPS, pulses, 2 * freqs), bf16),
            pltpu.VMEM((chunks, freqs, width), bf16),
            pltpu.VMEM((rows * maps, 2 * stacked), bf16),
            pltpu.VMEM((2, 2 * pulses, freqs), bf16),
            pltpu.VMEM((chunks, 2, 2 * stacked, width), bf16),
            pltpu.VMEM((columns, columns), bf16),
            pltpu.VMEM((chunks, rows, width), bf16),
            pltpu.VMEM((chunks, rows, width), bf16),
            pltpu.VMEM((chunks, rows, width), f32),
            pltpu.VMEM((chunks, slots, width), bf16),
            pltpu.VMEM((chunks, slots, width), bf16),
            pltpu.VMEM((slots, rows), bf16),
            pltpu.VMEM((blk, 1, LANES), f32),
            pltpu.VMEM((blk, 1, LANES), f32),
            pltpu.VMEM((slots, columns), f32),
            pltpu.VMEM((slots, columns), f32),
            dma((7,)), dma((STOPS,)), dma((chunks,)), dma((chunks,)),
            dma((chunks,)), dma((chunks,)), dma, dma,
        ],
        compiler_params=pltpu.CompilerParams(
            collective_id=0, has_side_effects=True, vmem_limit_bytes=60 * 2**20),
    )(
        phase_history[0, 0], tile_curvature, interp_weights[0],
        strip_tiles[0, 0].reshape(1, rows), row_offsets[0],
        tile_owner.reshape(1, blk),
    )
    return jnp.maximum(out, 0.0).reshape(1, 1, MAPH, columns)


def solution(mesh):
    in_specs = (
        P("blk", "map", None, None),
        P("blk"),
        P("blk", None, None),
        P("blk", "map", None, None),
        P("blk", "map", None),
        P(),
    )
    out_specs = P("blk", "map", None, None)
    return jax.shard_map(body, mesh=mesh, in_specs=in_specs, out_specs=out_specs, check_vma=False)
```
